512 devices in a mesh: seq: 128 (over z, y, core), rep: 4 (over x).
Axes of the slice: x: 4, y: 8, z: 8, core: 2. Of those that a mesh axis runs over, the one named last changes fastest.
Arguments:
- tokens: bfloat16 [16384, 2048], P('seq'), may hold values from -6 to 6
- norm_gain: float32 [2048], replicated, may hold values from 0.25 to 1.75
- refusal_dir: float32 [2048], replicated, may hold values from -6 to 6
- expert_ids: int32 [16384, 8], P('seq'), may hold values from 0 to 127, as said below
- gate_probs: float32 [16384, 8], P('seq'), may hold values from 0.05 to 0.5
- w_gate: bfloat16 [128, 768, 2048], P('seq', 'rep'), may hold values from -0.125 to 0.125
- w_up: bfloat16 [128, 768, 2048], P('seq', 'rep'), may hold values from -0.125 to 0.125
- w_down: bfloat16 [128, 768, 2048], P('seq', 'rep'), may hold values from -0.21875 to 0.21875
Outputs:
- ablated: bfloat16 [16384, 2048], P('seq', 'rep')
The draws below stay inside these ranges and needn't reach their ends.
Inputs may be any that keep to these rules, and one draw needn't show every extreme that they name: `expert_ids`: each row names 8 different experts. Among the 128 rows of one device no expert is named more than 12 times, and some expert is named exactly 12 times in the rows of every device.
All inputs are finite; a program needn't handle non-finite values.
Results may differ from the reference program's by a relative error of at most 0.0095.
Values may be sent and summed in bfloat16 or wider, within the bound.
A program may use at most 128 MiB of HBM per device.

```python
import math
import jax
import jax.numpy as jnp
from jax import lax

D = 2048
HID = 768
EXPERTS = 128
TOP = 8
TOK_DEV = 128
TOKENS = 16384
CAP = 12
N_SEQ = 128
N_REP = 4


def draw_expert_ids(key, part):
    blocks = TOKENS // TOK_DEV
    slot_count = TOK_DEV * TOP
    mean_load = slot_count // EXPERTS
    quarter_count = EXPERTS // 4
    low_count = EXPERTS - 2 * quarter_count
    ranking = jax.random.permutation(jax.random.fold_in(key, 7), EXPERTS).astype(jnp.int32)

    def one_block(block_key):
        key_a = jax.random.fold_in(block_key, 1)
        key_b = jax.random.fold_in(block_key, 2)
        key_c = jax.random.fold_in(block_key, 3)
        key_d = jax.random.fold_in(block_key, 4)
        others = jax.random.permutation(key_a, ranking[quarter_count:])
        signs = jax.random.randint(key_b, (low_count // 2,), 0, 2).astype(jnp.int32)
        offsets = jnp.stack([signs, -signs], axis=1).reshape(low_count)
        order_ids = jnp.concatenate([ranking[:quarter_count], others])
        loads = jnp.concatenate([jnp.full((quarter_count,), 3 * mean_load // 2, jnp.int32), jnp.full((quarter_count,), mean_load, jnp.int32), 3 * mean_load // 4 + offsets])
        shuffle = jax.random.permutation(key_c, EXPERTS).astype(jnp.int32)
        order_ids = order_ids[shuffle]
        loads = loads[shuffle]
        ends = jnp.cumsum(loads).astype(jnp.int32)
        slot_iota = jnp.arange(slot_count, dtype=jnp.int32)
        run_of = jnp.searchsorted(ends, slot_iota, side='right').astype(jnp.int32)
        expert_of = order_ids[run_of]
        token_perm = jax.random.permutation(key_d, TOK_DEV).astype(jnp.int32)
        chosen = jnp.zeros((TOK_DEV, TOP), jnp.int32)
        return chosen.at[token_perm[slot_iota % TOK_DEV], slot_iota // TOK_DEV].set(expert_of)
    block_keys = jax.random.split(jax.random.fold_in(key, 11), blocks)
    return jax.vmap(one_block)(block_keys).reshape(TOKENS, TOP)


def steps_of(stream_key, dims, shards, smallest, top_value):
    loudness = 1.0
    for axis_at, shards_of in shards:
        steps = jax.random.uniform(jax.random.fold_in(jax.random.fold_in(stream_key, 6), axis_at), (shards_of,), jnp.float32, smallest / len(shards), top_value / len(shards))
        loudness = loudness * jnp.repeat(jnp.exp(steps), dims[axis_at] // shards_of).reshape((-1,) + (1,) * (len(dims) - 1 - axis_at))
    return loudness


def centred(own_key, dims, scale, most, cuts=(), kind=jnp.bfloat16):
    array = jax.random.normal(own_key, dims, jnp.float32) * scale
    if len(cuts) > 0:
        array = steps_of(own_key, dims, cuts, -0.22, 0.18) * array
    return jnp.clip(array, min=-most, max=most).astype(kind)


def setup_inputs(seed: int = 0) -> dict:
    keys = jax.random.split(jax.random.key(seed), 9)
    tokens = centred(keys[0], (TOKENS, D), 1.0, 6.0, ((0, 128),))
    norm_gain = jnp.clip(1.0 + 0.15 * jax.random.normal(keys[1], (D,), jnp.float32), 0.25, 1.75)
    refusal_dir = centred(keys[2], (D,), 1.0, 6.0, (), jnp.float32)
    expert_ids = draw_expert_ids(jax.random.fold_in(keys[8], 71), 0)
    gate_probs = jnp.clip(jnp.exp(math.log(0.5) - 2.3025851 * jax.random.uniform(keys[4], (TOKENS, TOP), jnp.float32) ** steps_of(keys[4], (TOKENS, TOP), ((0, 128),), -0.2, 0.2)), 0.05, 0.5)
    w_gate = centred(keys[5], (EXPERTS, HID, D), D ** -0.5, 0.125, ((0, 128), (1, 4)))
    w_up = centred(keys[6], (EXPERTS, HID, D), D ** -0.5, 0.125, ((0, 128), (1, 4)))
    w_down = centred(keys[7], (EXPERTS, HID, D), HID ** -0.5, 0.21875, ((0, 128), (1, 4)))
    return {"tokens": tokens, "norm_gain": norm_gain, "refusal_dir": refusal_dir, "expert_ids": expert_ids, "gate_probs": gate_probs, "w_gate": w_gate, "w_up": w_up, "w_down": w_down}


def reference(tokens, norm_gain, refusal_dir, expert_ids, gate_probs, w_gate, w_up, w_down):
    tokens_f32 = tokens.astype(jnp.float32)
    inv_rms = lax.rsqrt(lax.optimization_barrier(jnp.mean(tokens_f32 * tokens_f32, axis=1, keepdims=True)) + 1e-06)
    normed = (tokens_f32 * inv_rms * norm_gain).astype(jnp.bfloat16)
    slot_count = TOKENS * TOP
    flat_ids = expert_ids.reshape(slot_count)
    flat_probs = gate_probs.reshape(slot_count)
    rows_most = N_SEQ * CAP
    quarter_width = HID // N_REP

    def per_expert(mixed, expert):
        picked = jnp.nonzero(flat_ids == expert, size=rows_most, fill_value=slot_count)[0].astype(jnp.int32)
        filled = picked < slot_count
        where_at = jnp.where(filled, picked, 0).astype(jnp.int32)
        token_at = where_at // TOP
        weight_at = jnp.where(filled, flat_probs[where_at], jnp.float32(0.0))
        row_block = normed[token_at]
        gate_val = jnp.einsum('rd,fd->rf', row_block, w_gate[expert], preferred_element_type=jnp.float32)
        up_val = jnp.einsum('rd,fd->rf', row_block, w_up[expert], preferred_element_type=jnp.float32)
        hidden = (jax.nn.silu(gate_val) * up_val).astype(jnp.bfloat16)
        hidden_q = hidden.reshape(rows_most, N_REP, quarter_width).astype(jnp.float32)
        down_q = w_down[expert].reshape(N_REP, quarter_width, D).astype(jnp.float32)
        pieces = jnp.einsum('rqh,qhd->rqd', hidden_q, down_q).astype(jnp.bfloat16).astype(jnp.float32)
        expert_out = lax.optimization_barrier(jnp.sum(pieces, axis=1)) * weight_at[:, None]
        return (mixed.at[token_at].add(expert_out), None)
    mixed, _ = lax.scan(per_expert, jnp.zeros((TOKENS, D), jnp.float32), jnp.arange(EXPERTS, dtype=jnp.int32))
    residual = tokens_f32 + mixed
    unit_dir = refusal_dir / jnp.sqrt(jnp.sum(refusal_dir * refusal_dir) + 1e-06)
    along_dir = lax.optimization_barrier(jnp.sum(residual * unit_dir, axis=1))
    return (residual - along_dir[:, None] * unit_dir).astype(jnp.bfloat16)
```

```python
import jax
import jax.numpy as jnp
from jax import lax
from jax.sharding import PartitionSpec as P

CAP = 12


def local(tokens, norm_gain, refusal_dir, expert_ids, gate_probs, w_gate, w_up, w_down):
    tok_rows, model_width = tokens.shape
    n_seq = lax.axis_size("seq")
    n_rep = lax.axis_size("rep")
    slots = CAP // n_rep
    part_width = model_width // n_rep
    rep = lax.axis_index("rep")
    wg = lax.all_gather(w_gate[0], "rep", axis=0, tiled=True)
    wu = lax.all_gather(w_up[0], "rep", axis=0, tiled=True)
    wd = lax.all_gather(w_down[0], "rep", axis=0, tiled=True)
    tokens_f32 = tokens.astype(jnp.float32)
    inv_rms = lax.rsqrt(jnp.mean(tokens_f32 * tokens_f32, axis=1, keepdims=True) + 1e-06)
    normed = (tokens_f32 * inv_rms * norm_gain).astype(jnp.bfloat16)
    same = expert_ids[:, :, None] == jnp.arange(n_seq, dtype=jnp.int32)[None, None, :]
    chosen = jnp.any(same, axis=1)
    probs = jnp.sum(jnp.where(same, gate_probs[:, :, None], 0.0), axis=1)
    order = jnp.arange(tok_rows)
    earlier = (order[:, None] > order[None, :]).astype(jnp.bfloat16)
    rank = jnp.dot(earlier, chosen.astype(jnp.bfloat16), preferred_element_type=jnp.float32)
    rank = rank.astype(jnp.int32) - slots * rep
    picked = jnp.stack([chosen & (rank == c) for c in range(slots)])
    sendbuf = jnp.einsum(
        "cte,td->ecd", picked.astype(jnp.bfloat16), normed, preferred_element_type=jnp.float32
    ).astype(jnp.bfloat16)
    arrived = lax.all_to_all(sendbuf, "seq", split_axis=0, concat_axis=0, tiled=True)
    gate_val = jnp.einsum("scd,fd->scf", arrived, wg, preferred_element_type=jnp.float32)
    up_val = jnp.einsum("scd,fd->scf", arrived, wu, preferred_element_type=jnp.float32)
    hidden = (jax.nn.silu(gate_val) * up_val).astype(jnp.bfloat16)
    pieces = jnp.einsum("scf,fd->scd", hidden, wd, preferred_element_type=jnp.float32).astype(
        jnp.bfloat16
    )
    returned = lax.all_to_all(pieces, "seq", split_axis=0, concat_axis=0, tiled=True)
    weight = jnp.where(picked, probs[None], 0.0)
    high = weight.astype(jnp.bfloat16)
    low = (weight - high.astype(jnp.float32)).astype(jnp.bfloat16)
    both = jnp.concatenate([high, low], axis=1)
    moe = jnp.einsum("cte,ecd->td", both, returned, preferred_element_type=jnp.float32)
    moe = moe[:tok_rows] + moe[tok_rows:]
    unit_dir = refusal_dir / jnp.sqrt(jnp.sum(refusal_dir * refusal_dir) + 1e-06)
    along_dir = jnp.sum(tokens_f32 * unit_dir, axis=1) + lax.psum(
        jnp.sum(moe * unit_dir, axis=1), "rep"
    )
    parts = moe.astype(jnp.bfloat16).reshape(tok_rows, n_rep, part_width).transpose(1, 0, 2)
    parts = lax.all_to_all(parts, "rep", split_axis=0, concat_axis=0, tiled=True)
    summed = jnp.sum(parts.astype(jnp.float32), axis=0)
    rep_offset = rep * part_width
    unit_slice = lax.dynamic_slice_in_dim(unit_dir, rep_offset, part_width, 0)
    own_tokens = lax.dynamic_slice_in_dim(tokens_f32, rep_offset, part_width, 1)
    residual = own_tokens + summed
    return (residual - along_dir[:, None] * unit_slice).astype(jnp.bfloat16)


def solution(mesh):
    placed = (
        P("seq", None),
        P(),
        P(),
        P("seq", None),
        P("seq", None),
        P("seq", "rep", None),
        P("seq", "rep", None),
        P("seq", "rep", None),
    )
    return jax.shard_map(
        local, mesh=mesh, in_specs=placed, out_specs=P("seq", "rep"), check_vma=False
    )
```

```python
import functools

import jax
import jax.numpy as jnp
from jax import lax
from jax.experimental import pallas as pl
from jax.experimental.pallas import tpu as pltpu
from jax.sharding import PartitionSpec as P

CAP = 12
LANES = 128
MESH = pl.DeviceIdType.MESH
F32 = jnp.float32
BF16 = jnp.bfloat16


def dot(a, b, dims):
    return lax.dot_general(a, b, (dims, ((), ())), preferred_element_type=F32)


def kernel(
    n_seq, n_rep, hops,
    tok, gain, direc, ids, ids_t, probs, wg, wu, wd,
    out,
    wbuf, stage, rows, send1, recv1, send2, recv2, hid, comb, unit, moe, part_out, part_in, dot_out, dot_in,
    loc, own, sx, rx, sf, rf, s1, r1, s2, r2, sp, rp, sd, rd,
):
    me = lax.axis_index("seq")
    rep = lax.axis_index("rep")
    tok_rows, width = tok.shape
    n_exp = n_seq
    slots = CAP // n_rep
    cols = width // LANES
    units = wg.shape[0]
    part = width // n_rep
    n_rows = n_exp * slots
    right = lax.rem(rep + 1, n_rep)
    left = lax.rem(rep + n_rep - 1, n_rep)
    far = lax.rem(rep + 2, n_rep)
    weights = (wg, wu, wd)

    def peer_of(i):
        return lax.rem(me + i * hops, n_seq)

    barrier = pltpu.get_barrier_semaphore()

    def greet(i, carry):
        pl.semaphore_signal(barrier, inc=1, device_id=(peer_of(i), rep), device_id_type=MESH)
        return carry

    for k in range(1, n_rep):
        pl.semaphore_signal(
            barrier, inc=1, device_id=(me, lax.rem(rep + k, n_rep)), device_id_type=MESH
        )
    lax.fori_loop(1, n_seq, greet, 0)

    def local_weight(t):
        return pltpu.make_async_copy(weights[t], wbuf.at[t, rep], loc.at[t])

    for t in range(3):
        local_weight(t).start()

    pl.semaphore_wait(barrier, n_seq - 1 + n_rep - 1)

    def direct(t, way):
        return pltpu.make_async_remote_copy(
            src_ref=weights[t],
            dst_ref=wbuf.at[t, rep],
            send_sem=sx.at[t, way],
            recv_sem=rx.at[t, way],
            device_id=(me, (right, left)[way]),
            device_id_type=MESH,
        )

    half = units // 2

    def forward(t, way):
        shard = wbuf.at[t, (left, right)[way], pl.ds(way * half, half)]
        return pltpu.make_async_remote_copy(
            src_ref=shard,
            dst_ref=shard,
            send_sem=sf.at[t, way],
            recv_sem=rf.at[t, way],
            device_id=(me, (right, left)[way]),
            device_id_type=MESH,
        )

    for t in range(2):
        for way in range(2):
            direct(t, way).start()

    tokens = tok[...].astype(F32)
    inv = lax.rsqrt(jnp.mean(tokens * tokens, axis=1, keepdims=True) + 1e-06)
    normed = (tokens * inv * gain[...]).astype(BF16)
    direction = direc[...]
    unit_dir = direction / jnp.sqrt(jnp.sum(direction * direction, axis=1, keepdims=True) + 1e-06)
    unit[...] = unit_dir

    top = ids.shape[1]
    sub = lax.broadcasted_iota(jnp.int32, (n_exp, tok_rows), 0)
    lane = lax.broadcasted_iota(jnp.int32, (n_exp, tok_rows), 1)
    chosen_t = jnp.zeros((n_exp, tok_rows), F32)
    chosen = jnp.zeros((tok_rows, n_exp), F32)
    prob = jnp.zeros((tok_rows, n_exp), F32)
    for k in range(top):
        chosen_t = jnp.where(ids_t[k : k + 1, :] == sub, 1.0, chosen_t)
        same = ids[:, k : k + 1] == lane
        chosen = jnp.where(same, 1.0, chosen)
        prob = jnp.where(same, probs[:, k : k + 1], prob)
    rank_t = dot(chosen_t.astype(BF16), (sub < lane).astype(F32).astype(BF16), ((1,), (0,)))
    rank = dot((lane < sub).astype(F32).astype(BF16), chosen.astype(BF16), ((1,), (0,)))
    first = rep * slots
    rank_t = rank_t.astype(jnp.int32) - first
    rank = rank.astype(jnp.int32) - first
    for c in range(slots):
        pick_t = jnp.where(rank_t == c, chosen_t, 0.0).astype(BF16)
        block = dot(pick_t, normed, ((1,), (0,)))
        for j in range(cols):
            stage[pl.ds(c * cols + j, n_exp, stride=slots * cols), :] = block[
                :, j * LANES : (j + 1) * LANES
            ]
        weight = jnp.where(rank == c, prob, 0.0) * chosen
        high = weight.astype(BF16)
        comb[0:tok_rows, c * n_exp : (c + 1) * n_exp] = high
        comb[tok_rows : 2 * tok_rows, c * n_exp : (c + 1) * n_exp] = (
            weight - high.astype(F32)
        ).astype(BF16)

    step = 8
    message = slots * cols

    def pack(dst):
        def body(b, carry):
            at = pl.multiple_of(b * step, step)
            block = stage[pl.ds(pl.multiple_of(b * (step * message), 16), step * message), :]
            dst[pl.ds(at, step)] = block.astype(BF16).reshape(step, message, LANES)
            return carry

        lax.fori_loop(0, n_exp // step, body, 0)

    def unpack(src):
        def body(b, carry):
            at = pl.multiple_of(b * step, step)
            block = src[pl.ds(at, step)].astype(F32).reshape(step * message, LANES)
            stage[pl.ds(pl.multiple_of(b * (step * message), 16), step * message), :] = block
            return carry

        lax.fori_loop(0, n_exp // step, body, 0)

    def exchange(src, dst, send_sem, recv_sem):
        mine = pltpu.make_async_copy(src.at[me], dst.at[me], own)

        def to(i, carry):
            peer = peer_of(i)
            pltpu.make_async_remote_copy(
                src_ref=src.at[peer],
                dst_ref=dst.at[me],
                send_sem=send_sem,
                recv_sem=recv_sem,
                device_id=(peer, rep),
                device_id_type=MESH,
            ).start()
            return carry

        mine.start()
        lax.fori_loop(1, n_seq, to, 0)
        return mine

    def settle(src, dst, send_sem, recv_sem):
        return pltpu.make_async_remote_copy(
            src_ref=src.at[pl.ds(0, n_seq - 1)],
            dst_ref=dst.at[pl.ds(0, n_seq - 1)],
            send_sem=send_sem,
            recv_sem=recv_sem,
            device_id=(lax.rem(me + 1, n_seq), rep),
            device_id_type=MESH,
        )

    pack(send1)
    mine = exchange(send1, recv1, s1, r1)

    for t in range(2):
        for way in range(2):
            direct(t, way).wait_recv()
            forward(t, way).start()
    for way in range(2):
        direct(2, way).start()

    mine.wait()
    settle(send1, recv1, s1, r1).wait_recv()
    unpack(recv1)
    for j in range(cols):
        rows[:, j * LANES : (j + 1) * LANES] = stage[pl.ds(j, n_rows, stride=cols), :].astype(BF16)

    def gate_up(q):
        x = rows[...]
        g = dot(x, wbuf[0, q], ((1,), (1,)))
        u = dot(x, wbuf[1, q], ((1,), (1,)))
        hid[q] = (g / (1.0 + jnp.exp(-g)) * u).astype(BF16)

    for t in range(3):
        local_weight(t).wait()

    def near(i, carry):
        gate_up(lax.rem(left + i, n_rep))
        return carry

    lax.fori_loop(0, 3, near, 0)
    for way in range(2):
        direct(2, way).wait_recv()
        forward(2, way).start()
    for t in range(2):
        for way in range(2):
            forward(t, way).wait_recv()
    gate_up(far)
    for way in range(2):
        forward(2, way).wait_recv()

    tile = 2 * LANES

    def down(n, carry):
        at = pl.multiple_of(n * tile, tile)
        acc = dot(hid[0], wbuf[2, 0, :, pl.ds(at, tile)], ((1,), (0,)))
        for q in range(1, n_rep):
            acc += dot(hid[q], wbuf[2, q, :, pl.ds(at, tile)], ((1,), (0,)))
        stage[pl.ds(2 * n, n_rows, stride=cols), :] = acc[:, :LANES]
        stage[pl.ds(2 * n + 1, n_rows, stride=cols), :] = acc[:, LANES:]
        return carry

    lax.fori_loop(0, width // tile, down, 0)
    pack(send2)
    mine = exchange(send2, recv2, s2, r2)

    base = jnp.sum(tok[...].astype(F32) * unit[...], axis=1, keepdims=True)

    mine.wait()
    settle(send2, recv2, s2, r2).wait_recv()
    unpack(recv2)
    for c in range(slots):
        for j in range(cols):
            rows[c * n_exp : (c + 1) * n_exp, j * LANES : (j + 1) * LANES] = stage[
                pl.ds(c * cols + j, n_exp, stride=message), :
            ].astype(BF16)
    along = jnp.zeros((tok_rows, 1), F32)
    for q in range(n_rep):
        m = dot(comb[...], rows[:, q * part : (q + 1) * part], ((1,), (0,)))
        m = m[:tok_rows] + m[tok_rows:]
        moe[q] = m
        part_out[q] = m.astype(BF16)
        along += jnp.sum(m * unit[:, q * part : (q + 1) * part], axis=1, keepdims=True)
    dot_out[...] = jnp.broadcast_to(along, (tok_rows, LANES)).T[:8]

    def give(k):
        q = lax.rem(rep + k, n_rep)
        return (
            pltpu.make_async_remote_copy(
                src_ref=part_out.at[q],
                dst_ref=part_in.at[k - 1],
                send_sem=sp.at[k - 1],
                recv_sem=rp.at[k - 1],
                device_id=(me, q),
                device_id_type=MESH,
            ),
            pltpu.make_async_remote_copy(
                src_ref=dot_out,
                dst_ref=dot_in.at[k - 1],
                send_sem=sd.at[k - 1],
                recv_sem=rd.at[k - 1],
                device_id=(me, q),
                device_id_type=MESH,
            ),
        )

    for k in (2, 1, 3):
        for copy in give(k):
            copy.start()
    mine_part = pl.ds(pl.multiple_of(rep * part, part), part)
    residual = tok[:, mine_part].astype(F32) + moe[rep]
    total = dot_out[...]
    for k in range(1, n_rep):
        for copy in give(k):
            copy.wait_recv()
        residual += part_in[k - 1].astype(F32)
        total += dot_in[k - 1]
    total = jnp.broadcast_to(total[0:1], (LANES, tok_rows)).T[:, 0:1] + base
    out[...] = (residual - total * unit[:, mine_part]).astype(BF16)

    for t in range(3):
        for way in range(2):
            direct(t, way).wait_send()
            forward(t, way).wait_send()
    settle(send1, recv1, s1, r1).wait_send()
    settle(send2, recv2, s2, r2).wait_send()
    for k in range(1, n_rep):
        for copy in give(k):
            copy.wait_send()


def local(tokens, norm_gain, refusal_dir, expert_ids, gate_probs, w_gate, w_up, w_down):
    tok_rows, width = tokens.shape
    n_seq = lax.axis_size("seq")
    n_rep = lax.axis_size("rep")
    slots = CAP // n_rep
    units = w_gate.shape[1]
    cols = width // LANES
    message = slots * cols
    part = width // n_rep
    vmem = pl.BlockSpec(memory_space=pltpu.VMEM)
    whole = pl.BlockSpec(memory_space=pl.ANY)
    dma = pltpu.SemaphoreType.DMA
    return pl.pallas_call(
        functools.partial(kernel, n_seq, n_rep, 37 if n_seq > 37 else 1),
        name="moe",
        out_shape=jax.ShapeDtypeStruct((tok_rows, part), BF16),
        in_specs=[vmem] * 6 + [whole] * 3,
        out_specs=vmem,
        scratch_shapes=[
            pltpu.VMEM((3, n_rep, units, width), BF16),
            pltpu.VMEM((n_seq * message, LANES), F32),
            pltpu.VMEM((n_seq * slots, width), BF16),
            pltpu.VMEM((n_seq, message, LANES), BF16),
            pltpu.VMEM((n_seq, message, LANES), BF16),
            pltpu.VMEM((n_seq, message, LANES), BF16),
            pltpu.VMEM((n_seq, message, LANES), BF16),
            pltpu.VMEM((n_rep, n_seq * slots, units), BF16),
            pltpu.VMEM((2 * tok_rows, n_seq * slots), BF16),
            pltpu.VMEM((1, width), F32),
            pltpu.VMEM((n_rep, tok_rows, part), F32),
            pltpu.VMEM((n_rep, tok_rows, part), BF16),
            pltpu.VMEM((n_rep - 1, tok_rows, part), BF16),
            pltpu.VMEM((8, LANES), F32),
            pltpu.VMEM((n_rep - 1, 8, LANES), F32),
            dma((3,)),
            dma,
            dma((3, 2)),
            dma((3, 2)),
            dma((3, 2)),
            dma((3, 2)),
            dma,
            dma,
            dma,
            dma,
            dma((n_rep - 1,)),
            dma((n_rep - 1,)),
            dma((n_rep - 1,)),
            dma((n_rep - 1,)),
        ],
        compiler_params=pltpu.CompilerParams(
            collective_id=0, has_side_effects=True, vmem_limit_bytes=56 * 1024 * 1024
        ),
    )(
        tokens,
        norm_gain[None],
        refusal_dir[None],
        expert_ids,
        expert_ids.T,
        gate_probs,
        w_gate[0],
        w_up[0],
        w_down[0],
    )


def solution(mesh):
    placed = (
        P("seq", None),
        P(),
        P(),
        P("seq", None),
        P("seq", None),
        P("seq", "rep", None),
        P("seq", "rep", None),
        P("seq", "rep", None),
    )
    return jax.shard_map(
        local, mesh=mesh, in_specs=placed, out_specs=P("seq", "rep"), check_vma=False
    )
```

```python
import functools

import jax
import jax.numpy as jnp
from jax import lax
from jax.experimental import pallas as pl
from jax.experimental.pallas import tpu as pltpu
from jax.sharding import PartitionSpec as P

CAP = 12
CHUNKS = 2
LANES = 128
MESH = pl.DeviceIdType.MESH
F32 = jnp.float32
BF16 = jnp.bfloat16


def dot(a, b, dims):
    return lax.dot_general(a, b, (dims, ((), ())), preferred_element_type=F32)


def kernel(
    n_seq, n_rep, hops, group,
    tok, gain, direc, ids_t, probs_t, wg, wu, wd,
    out,
    wbuf, dbuf, stage, rows, send1, recv1, send2, recv2, hid, comb, unit, moe, part_out, part_in, dot_out, dot_in,
    met, loc, loc_d, own, sx, rx, sf, rf, sx_d, rx_d, sf_d, rf_d, s1, r1, s2, r2, sp, rp, sd, rd,
):
    me = lax.axis_index("seq")
    rep = lax.axis_index("rep")
    tok_rows, width = tok.shape
    n_exp = n_seq
    slots = CAP // n_rep
    cols = width // LANES
    units = wg.shape[0]
    part = width // n_rep
    n_rows = n_exp * slots
    chunks = dbuf.shape[0]
    sub = part // chunks
    wide = cols // chunks
    per = sub // LANES
    right = lax.rem(rep + 1, n_rep)
    left = lax.rem(rep + n_rep - 1, n_rep)
    far = lax.rem(rep + 2, n_rep)
    beside = (right, left)

    def peer_of(i):
        return lax.rem(me + i * hops, n_seq)

    n_groups = n_seq // group
    place = lax.rem(me, group)
    first_of = me - place
    barrier = pltpu.get_barrier_semaphore()

    def greet(sem, seq, q):
        pl.semaphore_signal(sem, inc=1, device_id=(seq, q), device_id_type=MESH)

    def greet_group(i, carry):
        greet(barrier, first_of + lax.rem(place + i, group), rep)
        return carry

    def counterpart(i):
        return lax.rem(me + i * group, n_seq)

    def greet_counterpart(i, carry):
        greet(barrier, counterpart(i), rep)
        return carry

    def meet(i, carry):
        greet(met, counterpart(i), rep)
        return carry

    for k in range(1, n_rep):
        greet(barrier, me, lax.rem(rep + k, n_rep))
    lax.fori_loop(1, n_groups, greet_counterpart, 0)
    lax.fori_loop(1, group, greet_group, 0)

    weights = (wg, wu)

    def local_weight(t):
        return pltpu.make_async_copy(weights[t], wbuf.at[t, rep], loc.at[t])

    def down_cols(i, q):
        return wd.at[:, pl.ds(q * part + i * sub, sub)]

    def local_down(i, q):
        return pltpu.make_async_copy(down_cols(i, q), dbuf.at[i, q, rep], loc_d.at[i, q])

    for t in range(2):
        local_weight(t).start()
    for i in range(chunks):
        for q in range(n_rep):
            local_down(i, q).start()

    pl.semaphore_wait(barrier, n_rep - 1 + n_groups - 1 + group - 1)

    half = units // 2

    def pass_on(src, dst, send_sem, recv_sem, way):
        return pltpu.make_async_remote_copy(
            src_ref=src,
            dst_ref=dst,
            send_sem=send_sem,
            recv_sem=recv_sem,
            device_id=(me, beside[way]),
            device_id_type=MESH,
        )

    def direct(t, way):
        return pass_on(weights[t], wbuf.at[t, rep], sx.at[t, way], rx.at[t, way], way)

    def forward(t, way):
        shard = wbuf.at[t, beside[1 - way], pl.ds(way * half, half)]
        return pass_on(shard, shard, sf.at[t, way], rf.at[t, way], way)

    def direct_down(i, q, way):
        return pass_on(
            down_cols(i, q), dbuf.at[i, q, rep], sx_d.at[i, q, way], rx_d.at[i, q, way], way
        )

    def forward_down(i, q, way):
        shard = dbuf.at[i, q, beside[1 - way], pl.ds(way * half, half)]
        return pass_on(shard, shard, sf_d.at[i, q, way], rf_d.at[i, q, way], way)

    ways = range(2)
    quarters = range(n_rep)
    for t in range(2):
        for way in ways:
            direct(t, way).start()

    lax.fori_loop(1, n_groups, meet, 0)

    tokens = tok[...].astype(F32)
    inv = lax.rsqrt(jnp.mean(tokens * tokens, axis=1, keepdims=True) + 1e-06)
    normed = (tokens * inv * gain[...]).astype(BF16)

    top = ids_t.shape[0]
    expert = lax.broadcasted_iota(jnp.int32, (n_exp, tok_rows), 0)
    token = lax.broadcasted_iota(jnp.int32, (n_exp, tok_rows), 1)
    chosen = jnp.zeros((n_exp, tok_rows), F32)
    prob = jnp.zeros((n_exp, tok_rows), F32)
    for k in range(top):
        same = ids_t[k : k + 1, :] == expert
        chosen = jnp.where(same, 1.0, chosen)
        prob = jnp.where(same, probs_t[k : k + 1, :], prob)
    rank = dot(chosen.astype(BF16), (expert < token).astype(F32).astype(BF16), ((1,), (0,)))
    rank = rank.astype(jnp.int32) - rep * slots
    message = slots * cols
    for c in range(slots):
        pick = jnp.where(rank == c, chosen, 0.0).astype(BF16)
        block = dot(pick, normed, ((1,), (0,)))
        for j in range(cols):
            stage[pl.ds(c * cols + j, n_exp, stride=message), :] = block[
                :, j * LANES : (j + 1) * LANES
            ]

    step = 8

    def pack(dst, size):
        def body(b, carry):
            at = pl.multiple_of(b * step, step)
            block = stage[pl.ds(pl.multiple_of(b * (step * size), 16), step * size), :]
            dst[pl.ds(at, step)] = block.astype(BF16).reshape(step, size, LANES)
            return carry

        lax.fori_loop(0, n_exp // step, body, 0)

    def unpack(src, size):
        def body(b, carry):
            at = pl.multiple_of(b * step, step)
            block = src[pl.ds(at, step)].astype(F32).reshape(step * size, LANES)
            stage[pl.ds(pl.multiple_of(b * (step * size), 16), step * size), :] = block
            return carry

        lax.fori_loop(0, n_exp // step, body, 0)

    def keep(src, dst, sem):
        return pltpu.make_async_copy(src.at[me], dst.at[me], sem)

    def exchange(src, dst, send_sem, recv_sem):
        def to(i, carry):
            peer = peer_of(i)
            pltpu.make_async_remote_copy(
                src_ref=src.at[peer],
                dst_ref=dst.at[me],
                send_sem=send_sem,
                recv_sem=recv_sem,
                device_id=(peer, rep),
                device_id_type=MESH,
            ).start()
            return carry

        lax.fori_loop(1, n_seq, to, 0)

    def settle(src, dst, send_sem, recv_sem):
        return pltpu.make_async_remote_copy(
            src_ref=src.at[pl.ds(0, n_seq - 1)],
            dst_ref=dst.at[pl.ds(0, n_seq - 1)],
            send_sem=send_sem,
            recv_sem=recv_sem,
            device_id=(lax.rem(me + 1, n_seq), rep),
            device_id_type=MESH,
        )

    pack(send1, message)
    pl.semaphore_wait(met, n_groups - 1)
    exchange(send1, recv1, s1, r1)
    keep(send1, recv1, own.at[0]).start()

    for t in range(2):
        for way in ways:
            direct(t, way).wait_recv()
            forward(t, way).start()
    for q in quarters:
        for way in ways:
            direct_down(0, q, way).start()

    for c in range(slots):
        weight = (jnp.where(rank == c, prob, 0.0) * chosen).T
        high = weight.astype(BF16)
        comb[0:tok_rows, c * n_exp : (c + 1) * n_exp] = high
        comb[tok_rows : 2 * tok_rows, c * n_exp : (c + 1) * n_exp] = (
            weight - high.astype(F32)
        ).astype(BF16)
    direction = direc[...]
    unit[...] = direction / jnp.sqrt(
        jnp.sum(direction * direction, axis=1, keepdims=True) + 1e-06
    )
    for t in range(2):
        local_weight(t).wait()
    for i in range(chunks):
        for q in quarters:
            local_down(i, q).wait()

    keep(send1, recv1, own.at[0]).wait()
    settle(send1, recv1, s1, r1).wait_recv()
    unpack(recv1, message)
    for j in range(cols):
        rows[:, j * LANES : (j + 1) * LANES] = stage[pl.ds(j, n_rows, stride=cols), :].astype(BF16)

    def gate_up(q):
        x = rows[...]
        g = dot(x, wbuf[0, q], ((1,), (1,)))
        u = dot(x, wbuf[1, q], ((1,), (1,)))
        hid[q] = (g / (1.0 + jnp.exp(-g)) * u).astype(BF16)

    def near(i, carry):
        gate_up(lax.rem(left + i, n_rep))
        return carry

    lax.fori_loop(0, 3, near, 0)
    for q in quarters:
        for way in ways:
            direct_down(0, q, way).wait_recv()
            forward_down(0, q, way).start()
    for t in range(2):
        for way in ways:
            forward(t, way).wait_recv()
    gate_up(far)

    size = slots * wide
    for i in range(chunks):
        for q in quarters:
            for way in ways:
                forward_down(i, q, way).wait_recv()
        if i + 1 < chunks:
            for q in quarters:
                for way in ways:
                    direct_down(i + 1, q, way).start()

        def down(q, carry):
            acc = dot(hid[0], dbuf[i, q, 0], ((1,), (0,)))
            for other in range(1, n_rep):
                acc += dot(hid[other], dbuf[i, q, other], ((1,), (0,)))
            for j in range(per):
                stage[pl.ds(per * q + j, n_rows, stride=wide), :] = acc[
                    :, j * LANES : (j + 1) * LANES
                ]
            return carry

        lax.fori_loop(0, n_rep, down, 0)
        pack(send2.at[i], size)
        exchange(send2.at[i], recv2.at[i], s2.at[i], r2.at[i])
        keep(send2.at[i], recv2.at[i], own.at[1 + i]).start()
        if i + 1 < chunks:
            for q in quarters:
                for way in ways:
                    direct_down(i + 1, q, way).wait_recv()
                    forward_down(i + 1, q, way).start()

    base = jnp.sum(tok[...].astype(F32) * unit[...], axis=1, keepdims=True)

    def give(i, k):
        q = lax.rem(rep + k, n_rep)
        return pltpu.make_async_remote_copy(
            src_ref=part_out.at[i, q],
            dst_ref=part_in.at[i, k - 1],
            send_sem=sp.at[i, k - 1],
            recv_sem=rp.at[i, k - 1],
            device_id=(me, q),
            device_id_type=MESH,
        )

    def give_dot(k):
        return pltpu.make_async_remote_copy(
            src_ref=dot_out,
            dst_ref=dot_in.at[k - 1],
            send_sem=sd.at[k - 1],
            recv_sem=rd.at[k - 1],
            device_id=(me, lax.rem(rep + k, n_rep)),
            device_id_type=MESH,
        )

    along = jnp.zeros((tok_rows, 1), F32)
    for i in range(chunks):
        keep(send2.at[i], recv2.at[i], own.at[1 + i]).wait()
        settle(send2.at[i], recv2.at[i], s2.at[i], r2.at[i]).wait_recv()
        unpack(recv2.at[i], size)
        for c in range(slots):
            for j in range(wide):
                rows[c * n_exp : (c + 1) * n_exp, j * LANES : (j + 1) * LANES] = stage[
                    pl.ds(c * wide + j, n_exp, stride=size), :
                ].astype(BF16)
        for q in quarters:
            m = dot(comb[...], rows[:, q * sub : (q + 1) * sub], ((1,), (0,)))
            m = m[:tok_rows] + m[tok_rows:]
            moe[i, q] = m
            part_out[i, q] = m.astype(BF16)
            at = q * part + i * sub
            along += jnp.sum(m * unit[:, at : at + sub], axis=1, keepdims=True)
        for k in (2, 1, 3):
            give(i, k).start()
    dot_out[...] = jnp.broadcast_to(along, (tok_rows, LANES)).T[:8]
    for k in (2, 1, 3):
        give_dot(k).start()

    total = dot_out[...]
    for k in range(1, n_rep):
        give_dot(k).wait_recv()
        total += dot_in[k - 1]
    total = jnp.broadcast_to(total[0:1], (LANES, tok_rows)).T[:, 0:1] + base
    for i in range(chunks):
        mine = pl.ds(pl.multiple_of(rep * part + i * sub, sub), sub)
        residual = tok[:, mine].astype(F32) + moe[i, rep]
        for k in range(1, n_rep):
            give(i, k).wait_recv()
            residual += part_in[i, k - 1].astype(F32)
        out[:, i * sub : (i + 1) * sub] = (residual - total * unit[:, mine]).astype(BF16)

    for way in ways:
        for t in range(2):
            direct(t, way).wait_send()
            forward(t, way).wait_send()
        for i in range(chunks):
            for q in quarters:
                direct_down(i, q, way).wait_send()
                forward_down(i, q, way).wait_send()
    settle(send1, recv1, s1, r1).wait_send()
    for i in range(chunks):
        settle(send2.at[i], recv2.at[i], s2.at[i], r2.at[i]).wait_send()
        for k in range(1, n_rep):
            give(i, k).wait_send()
    for k in range(1, n_rep):
        give_dot(k).wait_send()


def local(tokens, norm_gain, refusal_dir, expert_ids, gate_probs, w_gate, w_up, w_down):
    tok_rows, width = tokens.shape
    n_seq = lax.axis_size("seq")
    n_rep = lax.axis_size("rep")
    slots = CAP // n_rep
    units = w_gate.shape[1]
    cols = width // LANES
    message = slots * cols
    part = width // n_rep
    sub = part // CHUNKS
    vmem = pl.BlockSpec(memory_space=pltpu.VMEM)
    whole = pl.BlockSpec(memory_space=pl.ANY)
    dma = pltpu.SemaphoreType.DMA
    return pl.pallas_call(
        functools.partial(kernel, n_seq, n_rep, 37, 16),
        name="moe",
        out_shape=jax.ShapeDtypeStruct((tok_rows, part), BF16),
        in_specs=[vmem] * 5 + [whole] * 3,
        out_specs=vmem,
        scratch_shapes=[
            pltpu.VMEM((2, n_rep, units, width), BF16),
            pltpu.VMEM((CHUNKS, n_rep, n_rep, units, sub), BF16),
            pltpu.VMEM((n_seq * message, LANES), F32),
            pltpu.VMEM((n_seq * slots, width), BF16),
            pltpu.VMEM((n_seq, message, LANES), BF16),
            pltpu.VMEM((n_seq, message, LANES), BF16),
            pltpu.VMEM((CHUNKS, n_seq, message // CHUNKS, LANES), BF16),
            pltpu.VMEM((CHUNKS, n_seq, message // CHUNKS, LANES), BF16),
            pltpu.VMEM((n_rep, n_seq * slots, units), BF16),
            pltpu.VMEM((2 * tok_rows, n_seq * slots), BF16),
            pltpu.VMEM((1, width), F32),
            pltpu.VMEM((CHUNKS, n_rep, tok_rows, sub), F32),
            pltpu.VMEM((CHUNKS, n_rep, tok_rows, sub), BF16),
            pltpu.VMEM((CHUNKS, n_rep - 1, tok_rows, sub), BF16),
            pltpu.VMEM((8, LANES), F32),
            pltpu.VMEM((n_rep - 1, 8, LANES), F32),
            pltpu.SemaphoreType.REGULAR,
            dma((2,)),
            dma((CHUNKS, n_rep)),
            dma((1 + CHUNKS,)),
            dma((2, 2)),
            dma((2, 2)),
            dma((2, 2)),
            dma((2, 2)),
            dma((CHUNKS, n_rep, 2)),
            dma((CHUNKS, n_rep, 2)),
            dma((CHUNKS, n_rep, 2)),
            dma((CHUNKS, n_rep, 2)),
            dma,
            dma,
            dma((CHUNKS,)),
            dma((CHUNKS,)),
            dma((CHUNKS, n_rep - 1)),
            dma((CHUNKS, n_rep - 1)),
            dma((n_rep - 1,)),
            dma((n_rep - 1,)),
        ],
        compiler_params=pltpu.CompilerParams(
            collective_id=0, has_side_effects=True, vmem_limit_bytes=56 * 1024 * 1024
        ),
    )(
        tokens,
        norm_gain[None],
        refusal_dir[None],
        expert_ids.T,
        gate_probs.T,
        w_gate[0],
        w_up[0],
        w_down[0],
    )


def solution(mesh):
    placed = (
        P("seq", None),
        P(),
        P(),
        P("seq", None),
        P("seq", None),
        P("seq", "rep", None),
        P("seq", "rep", None),
        P("seq", "rep", None),
    )
    return jax.shard_map(
        local, mesh=mesh, in_specs=placed, out_specs=P("seq", "rep"), check_vma=False
    )
```

```python
import functools

import jax
import jax.numpy as jnp
from jax import lax
from jax.experimental import pallas as pl
from jax.experimental.pallas import tpu as pltpu
from jax.sharding import PartitionSpec as P

CAP = 12
CHUNKS = 2
LANES = 128
MESH = pl.DeviceIdType.MESH
F32 = jnp.float32
BF16 = jnp.bfloat16


def dot(a, b, dims):
    return lax.dot_general(a, b, (dims, ((), ())), preferred_element_type=F32)


def kernel(
    n_seq, n_rep, hops, group,
    tok, gain, direc, ids_t, probs_t, wg, wu, wd,
    out,
    wbuf, dbuf, stage, rows, send1, recv1, send2, recv2, hid, comb, unit, moe, part_out, part_in, dot_out, dot_in,
    met, loc, loc_d, own, sx, rx, sf, rf, sx_d, rx_d, sf_d, rf_d, s1, r1, s2, r2, sp, rp, sd, rd,
):
    me = lax.axis_index("seq")
    rep = lax.axis_index("rep")
    tok_rows, width = tok.shape
    n_exp = n_seq
    slots = CAP // n_rep
    cols = width // LANES
    units = wg.shape[0]
    part = width // n_rep
    n_rows = n_exp * slots
    chunks = dbuf.shape[0]
    sub = part // chunks
    wide = cols // chunks
    per = sub // LANES
    right = lax.rem(rep + 1, n_rep)
    left = lax.rem(rep + n_rep - 1, n_rep)
    far = lax.rem(rep + 2, n_rep)
    beside = (right, left)

    def peer_of(i):
        return lax.rem(me + i * hops, n_seq)

    n_groups = n_seq // group
    place = lax.rem(me, group)
    mine_at = me // group
    first_of = me - place
    barrier = pltpu.get_barrier_semaphore()

    def greet(sem, seq, q):
        pl.semaphore_signal(sem, inc=1, device_id=(seq, q), device_id_type=MESH)

    def greet_group(i, carry):
        greet(barrier, first_of + lax.rem(place + i, group), rep)
        return carry

    def below(far_by):
        return (mine_at + n_groups - far_by) // n_groups

    def above(far_by):
        return (2 * n_groups - 1 - far_by - mine_at) // n_groups

    def greet_line(sem, far_by):
        @pl.when(below(far_by) == 1)
        def _():
            greet(sem, me - far_by * group, rep)

        @pl.when(above(far_by) == 1)
        def _():
            greet(sem, me + far_by * group, rep)

    for k in range(1, n_rep):
        greet(barrier, me, lax.rem(rep + k, n_rep))
    greet_line(barrier, 1)
    lax.fori_loop(1, group, greet_group, 0)

    weights = (wg, wu)

    def local_weight(t):
        return pltpu.make_async_copy(weights[t], wbuf.at[t, rep], loc.at[t])

    def down_cols(i, q):
        return wd.at[:, pl.ds(q * part + i * sub, sub)]

    def local_down(i, q):
        return pltpu.make_async_copy(down_cols(i, q), dbuf.at[i, q, rep], loc_d.at[i, q])

    for t in range(2):
        local_weight(t).start()
    for i in range(chunks):
        for q in range(n_rep):
            local_down(i, q).start()

    pl.semaphore_wait(barrier, n_rep - 1 + group - 1 + below(1) + above(1))

    half = units // 2

    def pass_on(src, dst, send_sem, recv_sem, way):
        return pltpu.make_async_remote_copy(
            src_ref=src,
            dst_ref=dst,
            send_sem=send_sem,
            recv_sem=recv_sem,
            device_id=(me, beside[way]),
            device_id_type=MESH,
        )

    def direct(t, way):
        return pass_on(weights[t], wbuf.at[t, rep], sx.at[t, way], rx.at[t, way], way)

    def forward(t, way):
        shard = wbuf.at[t, beside[1 - way], pl.ds(way * half, half)]
        return pass_on(shard, shard, sf.at[t, way], rf.at[t, way], way)

    def direct_down(i, q, way):
        return pass_on(
            down_cols(i, q), dbuf.at[i, q, rep], sx_d.at[i, q, way], rx_d.at[i, q, way], way
        )

    def forward_down(i, q, way):
        shard = dbuf.at[i, q, beside[1 - way], pl.ds(way * half, half)]
        return pass_on(shard, shard, sf_d.at[i, q, way], rf_d.at[i, q, way], way)

    ways = range(2)
    quarters = range(n_rep)
    for t in range(2):
        for way in ways:
            direct(t, way).start()

    greet_line(met.at[0], 1)

    tokens = tok[...].astype(F32)
    inv = lax.rsqrt(jnp.mean(tokens * tokens, axis=1, keepdims=True) + 1e-06)
    normed = (tokens * inv * gain[...]).astype(BF16)

    top = ids_t.shape[0]
    expert = lax.broadcasted_iota(jnp.int32, (n_exp, tok_rows), 0)
    token = lax.broadcasted_iota(jnp.int32, (n_exp, tok_rows), 1)
    chosen = jnp.zeros((n_exp, tok_rows), F32)
    prob = jnp.zeros((n_exp, tok_rows), F32)
    for k in range(top):
        same = ids_t[k : k + 1, :] == expert
        chosen = jnp.where(same, 1.0, chosen)
        prob = jnp.where(same, probs_t[k : k + 1, :], prob)
    rank = dot(chosen.astype(BF16), (expert < token).astype(F32).astype(BF16), ((1,), (0,)))
    rank = rank.astype(jnp.int32) - rep * slots
    message = slots * cols
    for c in range(slots):
        pick = jnp.where(rank == c, chosen, 0.0).astype(BF16)
        block = dot(pick, normed, ((1,), (0,)))
        for j in range(cols):
            stage[pl.ds(c * cols + j, n_exp, stride=message), :] = block[
                :, j * LANES : (j + 1) * LANES
            ]

    step = 8

    def pack(dst, size):
        def body(b, carry):
            at = pl.multiple_of(b * step, step)
            block = stage[pl.ds(pl.multiple_of(b * (step * size), 16), step * size), :]
            dst[pl.ds(at, step)] = block.astype(BF16).reshape(step, size, LANES)
            return carry

        lax.fori_loop(0, n_exp // step, body, 0)

    def unpack(src, size):
        def body(b, carry):
            at = pl.multiple_of(b * step, step)
            block = src[pl.ds(at, step)].astype(F32).reshape(step * size, LANES)
            stage[pl.ds(pl.multiple_of(b * (step * size), 16), step * size), :] = block
            return carry

        lax.fori_loop(0, n_exp // step, body, 0)

    def keep(src, dst, sem):
        return pltpu.make_async_copy(src.at[me], dst.at[me], sem)

    def exchange(src, dst, send_sem, recv_sem):
        def to(i, carry):
            peer = peer_of(i)
            pltpu.make_async_remote_copy(
                src_ref=src.at[peer],
                dst_ref=dst.at[me],
                send_sem=send_sem,
                recv_sem=recv_sem,
                device_id=(peer, rep),
                device_id_type=MESH,
            ).start()
            return carry

        lax.fori_loop(1, n_seq, to, 0)

    def settle(src, dst, send_sem, recv_sem):
        return pltpu.make_async_remote_copy(
            src_ref=src.at[pl.ds(0, n_seq - 1)],
            dst_ref=dst.at[pl.ds(0, n_seq - 1)],
            send_sem=send_sem,
            recv_sem=recv_sem,
            device_id=(lax.rem(me + 1, n_seq), rep),
            device_id_type=MESH,
        )

    pack(send1, message)
    for at, far_by in enumerate((1, 2, 4)):
        if at:
            greet_line(met.at[at], far_by)
        pl.semaphore_wait(met.at[at], below(far_by) + above(far_by))
    exchange(send1, recv1, s1, r1)
    keep(send1, recv1, own.at[0]).start()

    for t in range(2):
        for way in ways:
            direct(t, way).wait_recv()
            forward(t, way).start()
    for q in quarters:
        for way in ways:
            direct_down(0, q, way).start()

    for c in range(slots):
        weight = (jnp.where(rank == c, prob, 0.0) * chosen).T
        high = weight.astype(BF16)
        comb[0:tok_rows, c * n_exp : (c + 1) * n_exp] = high
        comb[tok_rows : 2 * tok_rows, c * n_exp : (c + 1) * n_exp] = (
            weight - high.astype(F32)
        ).astype(BF16)
    direction = direc[...]
    unit[...] = direction / jnp.sqrt(
        jnp.sum(direction * direction, axis=1, keepdims=True) + 1e-06
    )
    for t in range(2):
        local_weight(t).wait()
    for i in range(chunks):
        for q in quarters:
            local_down(i, q).wait()

    keep(send1, recv1, own.at[0]).wait()
    settle(send1, recv1, s1, r1).wait_recv()
    unpack(recv1, message)
    for j in range(cols):
        rows[:, j * LANES : (j + 1) * LANES] = stage[pl.ds(j, n_rows, stride=cols), :].astype(BF16)

    def gate_up(q):
        x = rows[...]
        g = dot(x, wbuf[0, q], ((1,), (1,)))
        u = dot(x, wbuf[1, q], ((1,), (1,)))
        hid[q] = (g / (1.0 + jnp.exp(-g)) * u).astype(BF16)

    def near(i, carry):
        gate_up(lax.rem(left + i, n_rep))
        return carry

    lax.fori_loop(0, 3, near, 0)
    for q in quarters:
        for way in ways:
            direct_down(0, q, way).wait_recv()
            forward_down(0, q, way).start()
    for t in range(2):
        for way in ways:
            forward(t, way).wait_recv()
    gate_up(far)

    size = slots * wide
    for i in range(chunks):
        for q in quarters:
            for way in ways:
                forward_down(i, q, way).wait_recv()
        if i + 1 < chunks:
            for q in quarters:
                for way in ways:
                    direct_down(i + 1, q, way).start()

        def down(q, carry):
            acc = dot(hid[0], dbuf[i, q, 0], ((1,), (0,)))
            for other in range(1, n_rep):
                acc += dot(hid[other], dbuf[i, q, other], ((1,), (0,)))
            for j in range(per):
                stage[pl.ds(per * q + j, n_rows, stride=wide), :] = acc[
                    :, j * LANES : (j + 1) * LANES
                ]
            return carry

        lax.fori_loop(0, n_rep, down, 0)
        pack(send2.at[i], size)
        exchange(send2.at[i], recv2.at[i], s2.at[i], r2.at[i])
        keep(send2.at[i], recv2.at[i], own.at[1 + i]).start()
        if i + 1 < chunks:
            for q in quarters:
                for way in ways:
                    direct_down(i + 1, q, way).wait_recv()
                    forward_down(i + 1, q, way).start()

    base = jnp.sum(tok[...].astype(F32) * unit[...], axis=1, keepdims=True)

    def give(i, k):
        q = lax.rem(rep + k, n_rep)
        return pltpu.make_async_remote_copy(
            src_ref=part_out.at[i, q],
            dst_ref=part_in.at[i, k - 1],
            send_sem=sp.at[i, k - 1],
            recv_sem=rp.at[i, k - 1],
            device_id=(me, q),
            device_id_type=MESH,
        )

    def give_dot(k):
        return pltpu.make_async_remote_copy(
            src_ref=dot_out,
            dst_ref=dot_in.at[k - 1],
            send_sem=sd.at[k - 1],
            recv_sem=rd.at[k - 1],
            device_id=(me, lax.rem(rep + k, n_rep)),
            device_id_type=MESH,
        )

    along = jnp.zeros((tok_rows, 1), F32)
    for i in range(chunks):
        keep(send2.at[i], recv2.at[i], own.at[1 + i]).wait()
        settle(send2.at[i], recv2.at[i], s2.at[i], r2.at[i]).wait_recv()
        unpack(recv2.at[i], size)
        for c in range(slots):
            for j in range(wide):
                rows[c * n_exp : (c + 1) * n_exp, j * LANES : (j + 1) * LANES] = stage[
                    pl.ds(c * wide + j, n_exp, stride=size), :
                ].astype(BF16)
        for q in quarters:
            m = dot(comb[...], rows[:, q * sub : (q + 1) * sub], ((1,), (0,)))
            m = m[:tok_rows] + m[tok_rows:]
            moe[i, q] = m
            part_out[i, q] = m.astype(BF16)
            at = q * part + i * sub
            along += jnp.sum(m * unit[:, at : at + sub], axis=1, keepdims=True)
        for k in (2, 1, 3):
            give(i, k).start()
    dot_out[...] = jnp.broadcast_to(along, (tok_rows, LANES)).T[:8]
    for k in (2, 1, 3):
        give_dot(k).start()

    total = dot_out[...]
    for k in range(1, n_rep):
        give_dot(k).wait_recv()
        total += dot_in[k - 1]
    total = jnp.broadcast_to(total[0:1], (LANES, tok_rows)).T[:, 0:1] + base
    for i in range(chunks):
        mine = pl.ds(pl.multiple_of(rep * part + i * sub, sub), sub)
        residual = tok[:, mine].astype(F32) + moe[i, rep]
        for k in range(1, n_rep):
            give(i, k).wait_recv()
            residual += part_in[i, k - 1].astype(F32)
        out[:, i * sub : (i + 1) * sub] = (residual - total * unit[:, mine]).astype(BF16)

    for way in ways:
        for t in range(2):
            direct(t, way).wait_send()
            forward(t, way).wait_send()
        for i in range(chunks):
            for q in quarters:
                direct_down(i, q, way).wait_send()
                forward_down(i, q, way).wait_send()
    settle(send1, recv1, s1, r1).wait_send()
    for i in range(chunks):
        settle(send2.at[i], recv2.at[i], s2.at[i], r2.at[i]).wait_send()
        for k in range(1, n_rep):
            give(i, k).wait_send()
    for k in range(1, n_rep):
        give_dot(k).wait_send()


def local(tokens, norm_gain, refusal_dir, expert_ids, gate_probs, w_gate, w_up, w_down):
    tok_rows, width = tokens.shape
    n_seq = lax.axis_size("seq")
    n_rep = lax.axis_size("rep")
    slots = CAP // n_rep
    units = w_gate.shape[1]
    cols = width // LANES
    message = slots * cols
    part = width // n_rep
    sub = part // CHUNKS
    vmem = pl.BlockSpec(memory_space=pltpu.VMEM)
    whole = pl.BlockSpec(memory_space=pl.ANY)
    dma = pltpu.SemaphoreType.DMA
    return pl.pallas_call(
        functools.partial(kernel, n_seq, n_rep, 37, 16),
        name="moe",
        out_shape=jax.ShapeDtypeStruct((tok_rows, part), BF16),
        in_specs=[vmem] * 5 + [whole] * 3,
        out_specs=vmem,
        scratch_shapes=[
            pltpu.VMEM((2, n_rep, units, width), BF16),
            pltpu.VMEM((CHUNKS, n_rep, n_rep, units, sub), BF16),
            pltpu.VMEM((n_seq * message, LANES), F32),
            pltpu.VMEM((n_seq * slots, width), BF16),
            pltpu.VMEM((n_seq, message, LANES), BF16),
            pltpu.VMEM((n_seq, message, LANES), BF16),
            pltpu.VMEM((CHUNKS, n_seq, message // CHUNKS, LANES), BF16),
            pltpu.VMEM((CHUNKS, n_seq, message // CHUNKS, LANES), BF16),
            pltpu.VMEM((n_rep, n_seq * slots, units), BF16),
            pltpu.VMEM((2 * tok_rows, n_seq * slots), BF16),
            pltpu.VMEM((1, width), F32),
            pltpu.VMEM((CHUNKS, n_rep, tok_rows, sub), F32),
            pltpu.VMEM((CHUNKS, n_rep, tok_rows, sub), BF16),
            pltpu.VMEM((CHUNKS, n_rep - 1, tok_rows, sub), BF16),
            pltpu.VMEM((8, LANES), F32),
            pltpu.VMEM((n_rep - 1, 8, LANES), F32),
            pltpu.SemaphoreType.REGULAR((3,)),
            dma((2,)),
            dma((CHUNKS, n_rep)),
            dma((1 + CHUNKS,)),
            dma((2, 2)),
            dma((2, 2)),
            dma((2, 2)),
            dma((2, 2)),
            dma((CHUNKS, n_rep, 2)),
            dma((CHUNKS, n_rep, 2)),
            dma((CHUNKS, n_rep, 2)),
            dma((CHUNKS, n_rep, 2)),
            dma,
            dma,
            dma((CHUNKS,)),
            dma((CHUNKS,)),
            dma((CHUNKS, n_rep - 1)),
            dma((CHUNKS, n_rep - 1)),
            dma((n_rep - 1,)),
            dma((n_rep - 1,)),
        ],
        compiler_params=pltpu.CompilerParams(
            collective_id=0, has_side_effects=True, vmem_limit_bytes=56 * 1024 * 1024
        ),
    )(
        tokens,
        norm_gain[None],
        refusal_dir[None],
        expert_ids.T,
        gate_probs.T,
        w_gate[0],
        w_up[0],
        w_down[0],
    )


def solution(mesh):
    placed = (
        P("seq", None),
        P(),
        P(),
        P("seq", None),
        P("seq", None),
        P("seq", "rep", None),
        P("seq", "rep", None),
        P("seq", "rep", None),
    )
    return jax.shard_map(
        local, mesh=mesh, in_specs=placed, out_specs=P("seq", "rep"), check_vma=False
    )
```

```python
import functools

import jax
import jax.numpy as jnp
from jax import lax
from jax.experimental import pallas as pl
from jax.experimental.pallas import tpu as pltpu
from jax.sharding import PartitionSpec as P

CAP = 12
CHUNKS = 2
LANES = 128
MESH = pl.DeviceIdType.MESH
F32 = jnp.float32
BF16 = jnp.bfloat16


def dot(a, b, dims):
    return lax.dot_general(a, b, (dims, ((), ())), preferred_element_type=F32)


def kernel(
    n_seq, n_rep, hops, group,
    tok, gain, direc, ids_t, probs_t, wg, wu, wd,
    out,
    wbuf, dbuf, stage, rows, send1, recv1, send2, recv2, hid, comb, unit, moe, part_out, part_in, dot_out, dot_in,
    met, loc, loc_d, own, sx, rx, sf, rf, sx_d, rx_d, sf_d, rf_d, s1, r1, s2, r2, sp, rp, sd, rd,
):
    me = lax.axis_index("seq")
    rep = lax.axis_index("rep")
    tok_rows, width = tok.shape
    n_exp = n_seq
    slots = CAP // n_rep
    cols = width // LANES
    units = wg.shape[0]
    part = width // n_rep
    n_rows = n_exp * slots
    chunks = dbuf.shape[0]
    sub = part // chunks
    wide = cols // chunks
    per = sub // LANES
    right = lax.rem(rep + 1, n_rep)
    left = lax.rem(rep + n_rep - 1, n_rep)
    far = lax.rem(rep + 2, n_rep)
    beside = (right, left)

    def peer_of(i):
        return lax.rem(me + i * hops, n_seq)

    def source_of(i):
        return lax.rem(me + (n_seq - i) * hops, n_seq)

    n_groups = n_seq // group
    place = lax.rem(me, group)
    mine_at = me // group
    first_of = me - place
    barrier = pltpu.get_barrier_semaphore()

    def greet(sem, seq, q):
        pl.semaphore_signal(sem, inc=1, device_id=(seq, q), device_id_type=MESH)

    def greet_group(i, carry):
        greet(barrier, first_of + lax.rem(place + i, group), rep)
        return carry

    def below(far_by):
        return (mine_at + n_groups - far_by) // n_groups

    def above(far_by):
        return (2 * n_groups - 1 - far_by - mine_at) // n_groups

    def greet_line(sem, far_by):
        @pl.when(below(far_by) == 1)
        def _():
            greet(sem, me - far_by * group, rep)

        @pl.when(above(far_by) == 1)
        def _():
            greet(sem, me + far_by * group, rep)

    for k in range(1, n_rep):
        greet(barrier, me, lax.rem(rep + k, n_rep))
    greet_line(barrier, 1)
    lax.fori_loop(1, group, greet_group, 0)

    weights = (wg, wu)

    def local_weight(t):
        return pltpu.make_async_copy(weights[t], wbuf.at[t, rep], loc.at[t])

    steps = (
        ((0, 0, 0, sub), (0, 1, 0, LANES)),
        ((0, 1, LANES, sub - LANES), (0, 2, 0, sub), (0, 3, 0, sub)),
        tuple((1, q, 0, sub) for q in range(n_rep)),
    )
    pieces = sum(steps, ())

    def down_cols(p):
        i, q, lo, n = p
        return wd.at[:, pl.ds(q * part + i * sub + lo, n)]

    def local_down(p):
        i, q, lo, n = p
        return pltpu.make_async_copy(
            down_cols(p), dbuf.at[i, q, rep, :, pl.ds(lo, n)], loc_d.at[pieces.index(p)]
        )

    for t in range(2):
        local_weight(t).start()
    for p in pieces:
        local_down(p).start()

    pl.semaphore_wait(barrier, n_rep - 1 + group - 1 + below(1) + above(1))

    half = units // 2

    def pass_on(src, dst, send_sem, recv_sem, way):
        return pltpu.make_async_remote_copy(
            src_ref=src,
            dst_ref=dst,
            send_sem=send_sem,
            recv_sem=recv_sem,
            device_id=(me, beside[way]),
            device_id_type=MESH,
        )

    def direct(t, way):
        return pass_on(weights[t], wbuf.at[t, rep], sx.at[t, way], rx.at[t, way], way)

    def forward(t, way):
        shard = wbuf.at[t, beside[1 - way], pl.ds(way * half, half)]
        return pass_on(shard, shard, sf.at[t, way], rf.at[t, way], way)

    def direct_down(p, way):
        i, q, lo, n = p
        at = pieces.index(p)
        return pass_on(
            down_cols(p),
            dbuf.at[i, q, rep, :, pl.ds(lo, n)],
            sx_d.at[at, way],
            rx_d.at[at, way],
            way,
        )

    def forward_down(p, way):
        i, q, lo, n = p
        at = pieces.index(p)
        shard = dbuf.at[i, q, beside[1 - way], pl.ds(way * half, half), pl.ds(lo, n)]
        return pass_on(shard, shard, sf_d.at[at, way], rf_d.at[at, way], way)

    ways = range(2)
    quarters = range(n_rep)
    for t in range(2):
        for way in ways:
            direct(t, way).start()

    greet_line(met.at[0], 1)

    tokens = tok[...].astype(F32)
    inv = lax.rsqrt(jnp.mean(tokens * tokens, axis=1, keepdims=True) + 1e-06)
    normed = (tokens * inv * gain[...]).astype(BF16)

    top = ids_t.shape[0]
    expert = lax.broadcasted_iota(jnp.int32, (n_exp, tok_rows), 0)
    token = lax.broadcasted_iota(jnp.int32, (n_exp, tok_rows), 1)
    chosen = jnp.zeros((n_exp, tok_rows), F32)
    prob = jnp.zeros((n_exp, tok_rows), F32)
    for k in range(top):
        same = ids_t[k : k + 1, :] == expert
        chosen = jnp.where(same, 1.0, chosen)
        prob = jnp.where(same, probs_t[k : k + 1, :], prob)
    rank = dot(chosen.astype(BF16), (expert < token).astype(F32).astype(BF16), ((1,), (0,)))
    rank = rank.astype(jnp.int32) - rep * slots
    message = slots * cols
    for c in range(slots):
        pick = jnp.where(rank == c, chosen, 0.0).astype(BF16)
        block = dot(pick, normed, ((1,), (0,)))
        for j in range(cols):
            stage[pl.ds(c * cols + j, n_exp, stride=message), :] = block[
                :, j * LANES : (j + 1) * LANES
            ]

    step = 8
    block_rows = step * message

    def pack1(b, carry):
        block = stage[pl.ds(pl.multiple_of(b * block_rows, 16), block_rows), :]
        send1[pl.ds(b * step, step)] = block.astype(BF16).reshape(step, message, LANES)
        return carry

    lax.fori_loop(0, n_exp // step, pack1, 0)

    for at, far_by in enumerate((1, 2, 4)):
        if at:
            greet_line(met.at[at], far_by)
        pl.semaphore_wait(met.at[at], below(far_by) + above(far_by))

    span = n_seq // 2

    def rows_out(i, h):
        peer = peer_of(i)
        return pltpu.make_async_remote_copy(
            src_ref=send1.at[peer],
            dst_ref=recv1.at[i],
            send_sem=s1.at[h],
            recv_sem=r1.at[h],
            device_id=(peer, rep),
            device_id_type=MESH,
        )

    def rows_all(h):
        held = pl.ds(0, span - 1 + h)
        return pltpu.make_async_remote_copy(
            src_ref=send1.at[held],
            dst_ref=recv1.at[held],
            send_sem=s1.at[h],
            recv_sem=r1.at[h],
            device_id=(lax.rem(me + 1, n_seq), rep),
            device_id_type=MESH,
        )

    own_rows = pltpu.make_async_copy(send1.at[me], recv1.at[0], own.at[0])
    for h in range(2):

        def rows_to(i, carry):
            rows_out(i, h).start()
            return carry

        lax.fori_loop(1 - h + h * span, span + h * span, rows_to, 0)
    own_rows.start()

    for t in range(2):
        for way in ways:
            direct(t, way).wait_recv()
            forward(t, way).start()
    for p in steps[0]:
        for way in ways:
            direct_down(p, way).start()

    for c in range(slots):
        weight = (jnp.where(rank == c, prob, 0.0) * chosen).T
        high = weight.astype(BF16)
        comb[0:tok_rows, c * n_exp : (c + 1) * n_exp] = high
        comb[tok_rows : 2 * tok_rows, c * n_exp : (c + 1) * n_exp] = (
            weight - high.astype(F32)
        ).astype(BF16)
    direction = direc[...]
    unit[...] = direction / jnp.sqrt(
        jnp.sum(direction * direction, axis=1, keepdims=True) + 1e-06
    )
    for t in range(2):
        local_weight(t).wait()
    for p in pieces:
        local_down(p).wait()

    own_rows.wait()
    held = span * slots

    def gate_up(q, h):
        at = pl.ds(h * held, held)
        x = rows[at, :]
        g = dot(x, wbuf[0, q], ((1,), (1,)))
        u = dot(x, wbuf[1, q], ((1,), (1,)))
        hid[q, at, :] = (g / (1.0 + jnp.exp(-g)) * u).astype(BF16)

    for h in range(2):
        rows_all(h).wait_recv()

        def unpack1(b, carry):
            at = h * span + b * step
            block = recv1[pl.ds(at, step)].astype(F32).reshape(block_rows, LANES)
            stage[pl.ds(pl.multiple_of(at * message, 16), block_rows), :] = block
            return carry

        lax.fori_loop(0, span // step, unpack1, 0)
        for c in range(slots):
            for j in range(cols):
                rows[h * held + c * span : h * held + (c + 1) * span, j * LANES : (j + 1) * LANES] = (
                    stage[pl.ds(h * span * message + c * cols + j, span, stride=message), :]
                ).astype(BF16)

        def near(i, carry):
            gate_up(lax.rem(left + i, n_rep), h)
            return carry

        lax.fori_loop(0, 3, near, 0)

    def hand_on(k):
        for p in steps[k]:
            for way in ways:
                direct_down(p, way).wait_recv()
                forward_down(p, way).start()
        if k + 1 < len(steps):
            for p in steps[k + 1]:
                for way in ways:
                    direct_down(p, way).start()

    hand_on(0)
    for t in range(2):
        for way in ways:
            forward(t, way).wait_recv()
    for h in range(2):
        gate_up(far, h)

    size = slots * wide
    returns = ((0, 0, 8), (0, 8, size - 8), (1, 0, size))

    def down(i, q, lo, n):
        acc = dot(hid[0], dbuf[i, q, 0, :, lo : lo + n], ((1,), (0,)))
        for other in range(1, n_rep):
            acc += dot(hid[other], dbuf[i, q, other, :, lo : lo + n], ((1,), (0,)))
        for j in range(n // LANES):
            for h in range(2):
                for c in range(slots):
                    at = h * held + c * span
                    to = h * span * size + (per * q + lo // LANES + j) * slots + c
                    stage[pl.ds(to, span, stride=size), :] = acc[
                        at : at + span, j * LANES : (j + 1) * LANES
                    ]

    def back(k, i):
        chunk, lo, n = returns[k]
        at = pl.ds(lo, n)
        return pltpu.make_async_remote_copy(
            src_ref=send2.at[chunk, i, at],
            dst_ref=recv2.at[chunk, me, at],
            send_sem=s2.at[k],
            recv_sem=r2.at[k],
            device_id=(source_of(i), rep),
            device_id_type=MESH,
        )

    def back_all(k):
        chunk, lo, n = returns[k]
        most = pl.ds(0, n_seq - 1)
        return pltpu.make_async_remote_copy(
            src_ref=send2.at[chunk, most, pl.ds(lo, n)],
            dst_ref=recv2.at[chunk, most, pl.ds(lo, n)],
            send_sem=s2.at[k],
            recv_sem=r2.at[k],
            device_id=(lax.rem(me + 1, n_seq), rep),
            device_id_type=MESH,
        )

    def back_own(k):
        chunk, lo, n = returns[k]
        at = pl.ds(lo, n)
        return pltpu.make_async_copy(
            send2.at[chunk, 0, at], recv2.at[chunk, me, at], own.at[1 + k]
        )

    for k in range(len(steps)):
        chunk, lo, n = returns[k]
        for p in steps[k]:
            for way in ways:
                forward_down(p, way).wait_recv()
        if k < 2:
            for p in steps[k]:
                down(*p)
        else:
            lax.fori_loop(0, n_rep, lambda q, carry: (down(1, q, 0, sub), carry)[1], 0)

        def pack2(b, carry):
            for u in range(step):
                i = b * step + u
                block = stage[pl.ds(pl.multiple_of(i * size + lo, 8), n), :]
                send2[chunk, i, lo : lo + n, :] = block.astype(BF16)
            return carry

        lax.fori_loop(0, n_seq // step, pack2, 0)

        def back_to(i, carry):
            back(k, i).start()
            return carry

        lax.fori_loop(1, n_seq, back_to, 0)
        back_own(k).start()
        if k + 1 < len(steps):
            hand_on(k + 1)

    base = jnp.sum(tok[...].astype(F32) * unit[...], axis=1, keepdims=True)

    def give(i, k):
        q = lax.rem(rep + k, n_rep)
        return pltpu.make_async_remote_copy(
            src_ref=part_out.at[i, q],
            dst_ref=part_in.at[i, k - 1],
            send_sem=sp.at[i, k - 1],
            recv_sem=rp.at[i, k - 1],
            device_id=(me, q),
            device_id_type=MESH,
        )

    def give_dot(k):
        return pltpu.make_async_remote_copy(
            src_ref=dot_out,
            dst_ref=dot_in.at[k - 1],
            send_sem=sd.at[k - 1],
            recv_sem=rd.at[k - 1],
            device_id=(me, lax.rem(rep + k, n_rep)),
            device_id_type=MESH,
        )

    along = jnp.zeros((tok_rows, 1), F32)
    for i in range(chunks):
        for k in range(len(returns)):
            if returns[k][0] == i:
                back_own(k).wait()
                back_all(k).wait_recv()

        def unpack2(b, carry):
            block = recv2[i, pl.ds(b * step, step)].astype(F32).reshape(step * size, LANES)
            stage[pl.ds(pl.multiple_of(b * (step * size), 16), step * size), :] = block
            return carry

        lax.fori_loop(0, n_exp // step, unpack2, 0)
        for c in range(slots):
            for j in range(wide):
                rows[c * n_exp : (c + 1) * n_exp, j * LANES : (j + 1) * LANES] = stage[
                    pl.ds(j * slots + c, n_exp, stride=size), :
                ].astype(BF16)
        for q in quarters:
            m = dot(comb[...], rows[:, q * sub : (q + 1) * sub], ((1,), (0,)))
            m = m[:tok_rows] + m[tok_rows:]
            moe[i, q] = m
            part_out[i, q] = m.astype(BF16)
            at = q * part + i * sub
            along += jnp.sum(m * unit[:, at : at + sub], axis=1, keepdims=True)
        for k in (2, 1, 3):
            give(i, k).start()
    dot_out[...] = jnp.broadcast_to(along, (tok_rows, LANES)).T[:8]
    for k in (2, 1, 3):
        give_dot(k).start()

    total = dot_out[...]
    for k in range(1, n_rep):
        give_dot(k).wait_recv()
        total += dot_in[k - 1]
    total = jnp.broadcast_to(total[0:1], (LANES, tok_rows)).T[:, 0:1] + base
    for i in range(chunks):
        mine = pl.ds(pl.multiple_of(rep * part + i * sub, sub), sub)
        residual = tok[:, mine].astype(F32) + moe[i, rep]
        for k in range(1, n_rep):
            give(i, k).wait_recv()
            residual += part_in[i, k - 1].astype(F32)
        out[:, i * sub : (i + 1) * sub] = (residual - total * unit[:, mine]).astype(BF16)

    for way in ways:
        for t in range(2):
            direct(t, way).wait_send()
            forward(t, way).wait_send()
        for p in pieces:
            direct_down(p, way).wait_send()
            forward_down(p, way).wait_send()
    for h in range(2):
        rows_all(h).wait_send()
    for k in range(len(returns)):
        back_all(k).wait_send()
    for i in range(chunks):
        for k in range(1, n_rep):
            give(i, k).wait_send()
    for k in range(1, n_rep):
        give_dot(k).wait_send()


def local(tokens, norm_gain, refusal_dir, expert_ids, gate_probs, w_gate, w_up, w_down):
    tok_rows, width = tokens.shape
    n_seq = lax.axis_size("seq")
    n_rep = lax.axis_size("rep")
    slots = CAP // n_rep
    units = w_gate.shape[1]
    cols = width // LANES
    message = slots * cols
    part = width // n_rep
    sub = part // CHUNKS
    vmem = pl.BlockSpec(memory_space=pltpu.VMEM)
    whole = pl.BlockSpec(memory_space=pl.ANY)
    dma = pltpu.SemaphoreType.DMA
    return pl.pallas_call(
        functools.partial(kernel, n_seq, n_rep, 37, 16),
        name="moe",
        out_shape=jax.ShapeDtypeStruct((tok_rows, part), BF16),
        in_specs=[vmem] * 5 + [whole] * 3,
        out_specs=vmem,
        scratch_shapes=[
            pltpu.VMEM((2, n_rep, units, width), BF16),
            pltpu.VMEM((CHUNKS, n_rep, n_rep, units, sub), BF16),
            pltpu.VMEM((n_seq * message, LANES), F32),
            pltpu.VMEM((n_seq * slots, width), BF16),
            pltpu.VMEM((n_seq, message, LANES), BF16),
            pltpu.VMEM((n_seq, message, LANES), BF16),
            pltpu.VMEM((CHUNKS, n_seq, message // CHUNKS, LANES), BF16),
            pltpu.VMEM((CHUNKS, n_seq, message // CHUNKS, LANES), BF16),
            pltpu.VMEM((n_rep, n_seq * slots, units), BF16),
            pltpu.VMEM((2 * tok_rows, n_seq * slots), BF16),
            pltpu.VMEM((1, width), F32),
            pltpu.VMEM((CHUNKS, n_rep, tok_rows, sub), F32),
            pltpu.VMEM((CHUNKS, n_rep, tok_rows, sub), BF16),
            pltpu.VMEM((CHUNKS, n_rep - 1, tok_rows, sub), BF16),
            pltpu.VMEM((8, LANES), F32),
            pltpu.VMEM((n_rep - 1, 8, LANES), F32),
            pltpu.SemaphoreType.REGULAR((3,)),
            dma((2,)),
            dma((9,)),
            dma((4,)),
            dma((2, 2)),
            dma((2, 2)),
            dma((2, 2)),
            dma((2, 2)),
            dma((9, 2)),
            dma((9, 2)),
            dma((9, 2)),
            dma((9, 2)),
            dma((2,)),
            dma((2,)),
            dma((3,)),
            dma((3,)),
            dma((CHUNKS, n_rep - 1)),
            dma((CHUNKS, n_rep - 1)),
            dma((n_rep - 1,)),
            dma((n_rep - 1,)),
        ],
        compiler_params=pltpu.CompilerParams(
            collective_id=0, has_side_effects=True, vmem_limit_bytes=56 * 1024 * 1024
        ),
    )(
        tokens,
        norm_gain[None],
        refusal_dir[None],
        expert_ids.T,
        gate_probs.T,
        w_gate[0],
        w_up[0],
        w_down[0],
    )


def solution(mesh):
    placed = (
        P("seq", None),
        P(),
        P(),
        P("seq", None),
        P("seq", None),
        P("seq", "rep", None),
        P("seq", "rep", None),
        P("seq", "rep", None),
    )
    return jax.shard_map(
        local, mesh=mesh, in_specs=placed, out_specs=P("seq", "rep"), check_vma=False
    )
```

```python
import functools

import jax
import jax.numpy as jnp
from jax import lax
from jax.experimental import pallas as pl
from jax.experimental.pallas import tpu as pltpu
from jax.sharding import PartitionSpec as P

CAP = 12
CHUNKS = 2
LANES = 128
MESH = pl.DeviceIdType.MESH
F32 = jnp.float32
BF16 = jnp.bfloat16


def dot(a, b, dims):
    return lax.dot_general(a, b, (dims, ((), ())), preferred_element_type=F32)


def kernel(
    n_seq, n_rep, hops, group,
    tok, gain, direc, ids_t, probs_t, wg, wu, wd,
    out,
    wbuf, dbuf, stage, rows, send1, recv1, send2, recv2, hid, comb, unit, moe, part_out, part_in, dot_out, dot_in,
    met, loc, loc_d, own, sx, rx, sf, rf, sx_d, rx_d, sf_d, rf_d, s1, r1, s2, r2, sp, rp, sd, rd,
):
    me = lax.axis_index("seq")
    rep = lax.axis_index("rep")
    tok_rows, width = tok.shape
    n_exp = n_seq
    slots = CAP // n_rep
    cols = width // LANES
    units = wg.shape[0]
    part = width // n_rep
    n_rows = n_exp * slots
    chunks = dbuf.shape[0]
    sub = part // chunks
    wide = cols // chunks
    per = sub // LANES
    right = lax.rem(rep + 1, n_rep)
    left = lax.rem(rep + n_rep - 1, n_rep)
    far = lax.rem(rep + 2, n_rep)
    beside = (right, left)

    def peer_of(i):
        return lax.rem(me + i * hops, n_seq)

    def source_of(i):
        return lax.rem(me + (n_seq - i) * hops, n_seq)

    n_groups = n_seq // group
    place = lax.rem(me, group)
    mine_at = me // group
    first_of = me - place
    barrier = pltpu.get_barrier_semaphore()

    def greet(sem, seq, q):
        pl.semaphore_signal(sem, inc=1, device_id=(seq, q), device_id_type=MESH)

    def greet_group(i, carry):
        greet(barrier, first_of + lax.rem(place + i, group), rep)
        return carry

    def below(far_by):
        return (mine_at + n_groups - far_by) // n_groups

    def above(far_by):
        return (2 * n_groups - 1 - far_by - mine_at) // n_groups

    def greet_line(sem, far_by):
        @pl.when(below(far_by) == 1)
        def _():
            greet(sem, me - far_by * group, rep)

        @pl.when(above(far_by) == 1)
        def _():
            greet(sem, me + far_by * group, rep)

    for k in range(1, n_rep):
        greet(barrier, me, lax.rem(rep + k, n_rep))
    greet_line(barrier, 1)
    lax.fori_loop(1, group, greet_group, 0)

    weights = (wg, wu)

    def local_weight(t):
        return pltpu.make_async_copy(weights[t], wbuf.at[t, rep], loc.at[t])

    steps = (
        ((0, 0, 0, sub), (0, 1, 0, LANES)),
        ((0, 1, LANES, sub - LANES), (0, 2, 0, sub), (0, 3, 0, sub)),
        tuple((1, q, 0, sub) for q in range(n_rep - 1)),
        ((1, n_rep - 1, 0, sub),),
    )
    pieces = sum(steps, ())

    def down_cols(p):
        i, q, lo, n = p
        return wd.at[:, pl.ds(q * part + i * sub + lo, n)]

    def local_down(p):
        i, q, lo, n = p
        return pltpu.make_async_copy(
            down_cols(p), dbuf.at[i, q, rep, :, pl.ds(lo, n)], loc_d.at[pieces.index(p)]
        )

    for t in range(2):
        local_weight(t).start()
    for p in pieces:
        local_down(p).start()

    pl.semaphore_wait(barrier, n_rep - 1 + group - 1 + below(1) + above(1))

    half = units // 2

    def pass_on(src, dst, send_sem, recv_sem, way):
        return pltpu.make_async_remote_copy(
            src_ref=src,
            dst_ref=dst,
            send_sem=send_sem,
            recv_sem=recv_sem,
            device_id=(me, beside[way]),
            device_id_type=MESH,
        )

    def direct(t, way):
        return pass_on(weights[t], wbuf.at[t, rep], sx.at[t, way], rx.at[t, way], way)

    def forward(t, way):
        shard = wbuf.at[t, beside[1 - way], pl.ds(way * half, half)]
        return pass_on(shard, shard, sf.at[t, way], rf.at[t, way], way)

    def direct_down(p, way):
        i, q, lo, n = p
        at = pieces.index(p)
        return pass_on(
            down_cols(p),
            dbuf.at[i, q, rep, :, pl.ds(lo, n)],
            sx_d.at[at, way],
            rx_d.at[at, way],
            way,
        )

    def forward_down(p, way):
        i, q, lo, n = p
        at = pieces.index(p)
        shard = dbuf.at[i, q, beside[1 - way], pl.ds(way * half, half), pl.ds(lo, n)]
        return pass_on(shard, shard, sf_d.at[at, way], rf_d.at[at, way], way)

    ways = range(2)
    quarters = range(n_rep)
    for t in range(2):
        for way in ways:
            direct(t, way).start()

    greet_line(met.at[0], 1)

    tokens = tok[...].astype(F32)
    inv = lax.rsqrt(jnp.mean(tokens * tokens, axis=1, keepdims=True) + 1e-06)
    normed = (tokens * inv * gain[...]).astype(BF16)

    top = ids_t.shape[0]
    expert = lax.broadcasted_iota(jnp.int32, (n_exp, tok_rows), 0)
    token = lax.broadcasted_iota(jnp.int32, (n_exp, tok_rows), 1)
    chosen = jnp.zeros((n_exp, tok_rows), F32)
    prob = jnp.zeros((n_exp, tok_rows), F32)
    for k in range(top):
        same = ids_t[k : k + 1, :] == expert
        chosen = jnp.where(same, 1.0, chosen)
        prob = jnp.where(same, probs_t[k : k + 1, :], prob)
    rank = dot(chosen.astype(BF16), (expert < token).astype(F32).astype(BF16), ((1,), (0,)))
    rank = rank.astype(jnp.int32) - rep * slots
    message = slots * cols
    for c in range(slots):
        pick = jnp.where(rank == c, chosen, 0.0).astype(BF16)
        block = dot(pick, normed, ((1,), (0,)))
        for j in range(cols):
            stage[pl.ds(c * cols + j, n_exp, stride=message), :] = block[
                :, j * LANES : (j + 1) * LANES
            ]

    step = 8
    block_rows = step * message

    def pack1(b, carry):
        block = stage[pl.ds(pl.multiple_of(b * block_rows, 16), block_rows), :]
        send1[pl.ds(b * step, step)] = block.astype(BF16).reshape(step, message, LANES)
        return carry

    lax.fori_loop(0, n_exp // step, pack1, 0)

    for at, far_by in enumerate((1, 2, 4)):
        if at:
            greet_line(met.at[at], far_by)
        pl.semaphore_wait(met.at[at], below(far_by) + above(far_by))

    span = n_seq // 2

    def rows_out(i, h):
        peer = peer_of(i)
        return pltpu.make_async_remote_copy(
            src_ref=send1.at[peer],
            dst_ref=recv1.at[i],
            send_sem=s1.at[h],
            recv_sem=r1.at[h],
            device_id=(peer, rep),
            device_id_type=MESH,
        )

    def rows_all(h):
        held = pl.ds(0, span - 1 + h)
        return pltpu.make_async_remote_copy(
            src_ref=send1.at[held],
            dst_ref=recv1.at[held],
            send_sem=s1.at[h],
            recv_sem=r1.at[h],
            device_id=(lax.rem(me + 1, n_seq), rep),
            device_id_type=MESH,
        )

    own_rows = pltpu.make_async_copy(send1.at[me], recv1.at[0], own.at[0])
    for h in range(2):

        def rows_to(i, carry):
            rows_out(i, h).start()
            return carry

        lax.fori_loop(1 - h + h * span, span + h * span, rows_to, 0)
    own_rows.start()

    for t in range(2):
        for way in ways:
            direct(t, way).wait_recv()
            forward(t, way).start()
    for p in steps[0]:
        for way in ways:
            direct_down(p, way).start()

    for c in range(slots):
        weight = (jnp.where(rank == c, prob, 0.0) * chosen).T
        high = weight.astype(BF16)
        comb[0:tok_rows, c * n_exp : (c + 1) * n_exp] = high
        comb[tok_rows : 2 * tok_rows, c * n_exp : (c + 1) * n_exp] = (
            weight - high.astype(F32)
        ).astype(BF16)
    direction = direc[...]
    unit[...] = direction / jnp.sqrt(
        jnp.sum(direction * direction, axis=1, keepdims=True) + 1e-06
    )
    for t in range(2):
        local_weight(t).wait()
    for p in pieces:
        local_down(p).wait()

    own_rows.wait()
    held = span * slots

    def gate_up(q, h):
        at = pl.ds(h * held, held)
        x = rows[at, :]
        g = dot(x, wbuf[0, q], ((1,), (1,)))
        u = dot(x, wbuf[1, q], ((1,), (1,)))
        hid[q, at, :] = (g / (1.0 + jnp.exp(-g)) * u).astype(BF16)

    def send_down(k):
        for p in steps[k]:
            for way in ways:
                direct_down(p, way).start()

    def hand_on(k):
        for p in steps[k]:
            for way in ways:
                direct_down(p, way).wait_recv()
                forward_down(p, way).start()

    for h in range(2):
        rows_all(h).wait_recv()

        def unpack1(b, carry):
            at = h * span + b * step
            block = recv1[pl.ds(at, step)].astype(F32).reshape(block_rows, LANES)
            stage[pl.ds(pl.multiple_of(at * message, 16), block_rows), :] = block
            return carry

        lax.fori_loop(0, span // step, unpack1, 0)
        for c in range(slots):
            for j in range(cols):
                rows[h * held + c * span : h * held + (c + 1) * span, j * LANES : (j + 1) * LANES] = (
                    stage[pl.ds(h * span * message + c * cols + j, span, stride=message), :]
                ).astype(BF16)

        def near(i, carry):
            gate_up(lax.rem(left + i, n_rep), h)
            return carry

        lax.fori_loop(0, 3, near, 0)
        if h == 0:
            hand_on(0)

    for t in range(2):
        for way in ways:
            forward(t, way).wait_recv()
    send_down(1)
    for h in range(2):
        gate_up(far, h)

    size = slots * wide
    returns = ((0, 0, 8), (0, 8, size - 8), (1, 0, size - 8), (1, size - 8, 8))

    def down(i, q, lo, n):
        acc = dot(hid[0], dbuf[i, q, 0, :, lo : lo + n], ((1,), (0,)))
        for other in range(1, n_rep):
            acc += dot(hid[other], dbuf[i, q, other, :, lo : lo + n], ((1,), (0,)))
        for j in range(n // LANES):
            for h in range(2):
                for c in range(slots):
                    at = h * held + c * span
                    to = h * span * size + (per * q + lo // LANES + j) * slots + c
                    stage[pl.ds(to, span, stride=size), :] = acc[
                        at : at + span, j * LANES : (j + 1) * LANES
                    ]

    def back(k, i):
        chunk, lo, n = returns[k]
        at = pl.ds(lo, n)
        return pltpu.make_async_remote_copy(
            src_ref=send2.at[chunk, i, at],
            dst_ref=recv2.at[chunk, me, at],
            send_sem=s2.at[k],
            recv_sem=r2.at[k],
            device_id=(source_of(i), rep),
            device_id_type=MESH,
        )

    def back_all(k):
        chunk, lo, n = returns[k]
        most = pl.ds(0, n_seq - 1)
        return pltpu.make_async_remote_copy(
            src_ref=send2.at[chunk, most, pl.ds(lo, n)],
            dst_ref=recv2.at[chunk, most, pl.ds(lo, n)],
            send_sem=s2.at[k],
            recv_sem=r2.at[k],
            device_id=(lax.rem(me + 1, n_seq), rep),
            device_id_type=MESH,
        )

    def back_own(k):
        chunk, lo, n = returns[k]
        at = pl.ds(lo, n)
        return pltpu.make_async_copy(
            send2.at[chunk, 0, at], recv2.at[chunk, me, at], own.at[1 + k]
        )

    for k in range(len(steps)):
        chunk, lo, n = returns[k]
        for p in steps[k]:
            for way in ways:
                forward_down(p, way).wait_recv()
        for p in steps[k]:
            down(*p)

        def pack2(b, carry):
            for u in range(step):
                i = b * step + u
                block = stage[pl.ds(pl.multiple_of(i * size + lo, 8), n), :]
                send2[chunk, i, lo : lo + n, :] = block.astype(BF16)
            return carry

        lax.fori_loop(0, n_seq // step, pack2, 0)

        def back_to(i, carry):
            back(k, i).start()
            return carry

        lax.fori_loop(1, span, back_to, 0)
        if k + 1 < len(steps):
            hand_on(k + 1)
        if k + 2 < len(steps):
            send_down(k + 2)
        lax.fori_loop(span, n_seq, back_to, 0)
        back_own(k).start()

    base = jnp.sum(tok[...].astype(F32) * unit[...], axis=1, keepdims=True)

    def give(i, k):
        q = lax.rem(rep + k, n_rep)
        return pltpu.make_async_remote_copy(
            src_ref=part_out.at[i, q],
            dst_ref=part_in.at[i, k - 1],
            send_sem=sp.at[i, k - 1],
            recv_sem=rp.at[i, k - 1],
            device_id=(me, q),
            device_id_type=MESH,
        )

    def give_dot(k):
        return pltpu.make_async_remote_copy(
            src_ref=dot_out,
            dst_ref=dot_in.at[k - 1],
            send_sem=sd.at[k - 1],
            recv_sem=rd.at[k - 1],
            device_id=(me, lax.rem(rep + k, n_rep)),
            device_id_type=MESH,
        )

    along = jnp.zeros((tok_rows, 1), F32)

    def landed(i, lo, n):
        def body(b, carry):
            block = recv2[i, pl.ds(b * step, step), lo : lo + n, :].astype(F32)
            stage[pl.ds(pl.multiple_of(b * (step * n), 16), step * n), :] = block.reshape(
                step * n, LANES
            )
            return carry

        lax.fori_loop(0, n_exp // step, body, 0)

    landings = (
        (0, (0, 1), 0, size, range(n_rep)),
        (1, (2,), 0, size - 8, range(n_rep // 2)),
        (1, (3,), 8, size - 8, range(n_rep // 2, n_rep)),
    )
    for i, waits, lo, n, done in landings:
        for k in waits:
            back_own(k).wait()
            back_all(k).wait_recv()
        landed(i, lo, n)
        for j in range(per * done[0], per * done[-1] + per):
            for c in range(slots):
                rows[c * n_exp : (c + 1) * n_exp, j * LANES : (j + 1) * LANES] = stage[
                    pl.ds(j * slots + c - lo, n_exp, stride=n), :
                ].astype(BF16)
        for q in done:
            m = dot(comb[...], rows[:, q * sub : (q + 1) * sub], ((1,), (0,)))
            m = m[:tok_rows] + m[tok_rows:]
            moe[i, q] = m
            part_out[i, q] = m.astype(BF16)
            at = q * part + i * sub
            along += jnp.sum(m * unit[:, at : at + sub], axis=1, keepdims=True)
        for k in (2, 1, 3):
            if len(done) == n_rep:
                give(i, k).start()
            else:

                @pl.when(lax.rem(rep + k, n_rep) // len(done) == done[0] // len(done))
                def _():
                    give(i, k).start()

    dot_out[...] = jnp.broadcast_to(along, (tok_rows, LANES)).T[:8]
    for k in (2, 1, 3):
        give_dot(k).start()

    total = dot_out[...]
    for k in range(1, n_rep):
        give_dot(k).wait_recv()
        total += dot_in[k - 1]
    total = jnp.broadcast_to(total[0:1], (LANES, tok_rows)).T[:, 0:1] + base
    for i in range(chunks):
        mine = pl.ds(pl.multiple_of(rep * part + i * sub, sub), sub)
        residual = tok[:, mine].astype(F32) + moe[i, rep]
        for k in range(1, n_rep):
            give(i, k).wait_recv()
            residual += part_in[i, k - 1].astype(F32)
        out[:, i * sub : (i + 1) * sub] = (residual - total * unit[:, mine]).astype(BF16)

    for way in ways:
        for t in range(2):
            direct(t, way).wait_send()
            forward(t, way).wait_send()
        for p in pieces:
            direct_down(p, way).wait_send()
            forward_down(p, way).wait_send()
    for h in range(2):
        rows_all(h).wait_send()
    for k in range(len(returns)):
        back_all(k).wait_send()
    for i in range(chunks):
        for k in range(1, n_rep):
            give(i, k).wait_send()
    for k in range(1, n_rep):
        give_dot(k).wait_send()


def local(tokens, norm_gain, refusal_dir, expert_ids, gate_probs, w_gate, w_up, w_down):
    tok_rows, width = tokens.shape
    n_seq = lax.axis_size("seq")
    n_rep = lax.axis_size("rep")
    slots = CAP // n_rep
    units = w_gate.shape[1]
    cols = width // LANES
    message = slots * cols
    part = width // n_rep
    sub = part // CHUNKS
    vmem = pl.BlockSpec(memory_space=pltpu.VMEM)
    whole = pl.BlockSpec(memory_space=pl.ANY)
    dma = pltpu.SemaphoreType.DMA
    return pl.pallas_call(
        functools.partial(kernel, n_seq, n_rep, 37, 16),
        name="moe",
        out_shape=jax.ShapeDtypeStruct((tok_rows, part), BF16),
        in_specs=[vmem] * 5 + [whole] * 3,
        out_specs=vmem,
        scratch_shapes=[
            pltpu.VMEM((2, n_rep, units, width), BF16),
            pltpu.VMEM((CHUNKS, n_rep, n_rep, units, sub), BF16),
            pltpu.VMEM((n_seq * message, LANES), F32),
            pltpu.VMEM((n_seq * slots, width), BF16),
            pltpu.VMEM((n_seq, message, LANES), BF16),
            pltpu.VMEM((n_seq, message, LANES), BF16),
            pltpu.VMEM((CHUNKS, n_seq, message // CHUNKS, LANES), BF16),
            pltpu.VMEM((CHUNKS, n_seq, message // CHUNKS, LANES), BF16),
            pltpu.VMEM((n_rep, n_seq * slots, units), BF16),
            pltpu.VMEM((2 * tok_rows, n_seq * slots), BF16),
            pltpu.VMEM((1, width), F32),
            pltpu.VMEM((CHUNKS, n_rep, tok_rows, sub), F32),
            pltpu.VMEM((CHUNKS, n_rep, tok_rows, sub), BF16),
            pltpu.VMEM((CHUNKS, n_rep - 1, tok_rows, sub), BF16),
            pltpu.VMEM((8, LANES), F32),
            pltpu.VMEM((n_rep - 1, 8, LANES), F32),
            pltpu.SemaphoreType.REGULAR((3,)),
            dma((2,)),
            dma((9,)),
            dma((5,)),
            dma((2, 2)),
            dma((2, 2)),
            dma((2, 2)),
            dma((2, 2)),
            dma((9, 2)),
            dma((9, 2)),
            dma((9, 2)),
            dma((9, 2)),
            dma((2,)),
            dma((2,)),
            dma((4,)),
            dma((4,)),
            dma((CHUNKS, n_rep - 1)),
            dma((CHUNKS, n_rep - 1)),
            dma((n_rep - 1,)),
            dma((n_rep - 1,)),
        ],
        compiler_params=pltpu.CompilerParams(
            collective_id=0, has_side_effects=True, vmem_limit_bytes=56 * 1024 * 1024
        ),
    )(
        tokens,
        norm_gain[None],
        refusal_dir[None],
        expert_ids.T,
        gate_probs.T,
        w_gate[0],
        w_up[0],
        w_down[0],
    )


def solution(mesh):
    placed = (
        P("seq", None),
        P(),
        P(),
        P("seq", None),
        P("seq", None),
        P("seq", "rep", None),
        P("seq", "rep", None),
        P("seq", "rep", None),
    )
    return jax.shard_map(
        local, mesh=mesh, in_specs=placed, out_specs=P("seq", "rep"), check_vma=False
    )
```
